256 devices in a mesh: lat: 8 (over z), slab: 32 (over x, y, core).
Axes of the slice: x: 4, y: 4, z: 8, core: 2. Of those that a mesh axis runs over, the one named last changes fastest.
Arguments:
- field_state: float32 [8, 128, 128, 5, 128], P('lat', 'slab'), may hold values from -6 to 6
- cotangent: float32 [8, 128, 128, 5, 128], P('lat', None, 'slab'), may hold values from -6 to 6
- vertical_weight: float32 [8, 128, 128, 128], P('lat', 'slab'), may hold values from 0 to 1
- diffusion_inverse: float32 [8, 5, 128, 128], P('lat'), as said below
- source_row: int32 [8, 32, 8, 32, 4], P('lat', 'slab'), may hold values from 0 to 383, as said below
- dest_slot: int32 [8, 32, 512], P('lat', 'slab'), may hold values from 0 to 1023, as said below
Outputs:
- tangent_out: float32 [8, 128, 128, 5, 128], P('lat', None, 'slab')
- adjoint_out: float32 [8, 128, 128, 5, 128], P('lat', 'slab')
The draws below stay inside these ranges and needn't reach their ends.
Inputs may be any that keep to these rules, and one draw needn't show every extreme that they name: `source_row`: from one sender to one receiver at most 4 slots are used, the used ones first; unused slots hold 0. Every value is below (3) * 128. `dest_slot`: each device's arrival rows name distinct used slots, and every used slot aimed at that device is named once; some sender fills all 4 slots to a receiver in every draw. `diffusion_inverse`: dense matrices of order one.
All inputs are finite; a program needn't handle non-finite values.
Results may differ from the reference program's by a relative error of at most 0.00007.
Values sent between devices are 32-bit elements; how exact they have to be, the bound alone decides.
A program may use at most 128 MiB of HBM per device.

```python
import math
import jax
import jax.numpy as jnp
from jax import lax

F = 5
BW = 128
LEV_DEV = 4
BLOCKS = 128
LEV = 128
CAP = 4
N_LAT = 8
N_SLAB = 32


def routes(key):
    key = jax.random.fold_in(key, 7)
    key_base, key_perm, key_rows = jax.random.split(key, 3)
    devices_all = N_LAT * N_SLAB
    row_total = LEV_DEV * BLOCKS
    slot_total = devices_all * CAP
    ranks = jnp.arange(devices_all, dtype=jnp.int32)
    group_gap = jnp.abs(ranks[:, None] // N_SLAB - ranks[None, :] // N_SLAB)
    nearness = jnp.where(group_gap == 0, 2000, jnp.where(group_gap == 1, 1000, 0))
    itself = jnp.where(ranks[:, None] == ranks[None, :], 100000, 0)
    base = jax.random.randint(key_base, (devices_all, devices_all), 0, 1000) + nearness + itself
    slot_ids = jnp.arange(CAP, dtype=jnp.int32)
    scores = base[:, :, None] - 300 * slot_ids[None, None, :]
    flat_ids = ranks[:, None] * CAP + slot_ids[None, :]
    keyed = (scores * slot_total + flat_ids[None, :, :]).reshape(devices_all, slot_total)
    unused_vals, chosen = lax.top_k(keyed, row_total)
    chosen = chosen.astype(jnp.int32)

    def shuffle(key_row, row_ids):
        return jax.random.permutation(key_row, row_ids)
    dest_all = jax.vmap(shuffle)(jax.random.split(key_perm, devices_all), chosen)
    used = jnp.zeros((devices_all, slot_total), jnp.int32).at[ranks[:, None], chosen].set(1)
    picks = jax.random.randint(key_rows, (devices_all, slot_total), 0, (LEV_DEV - 1) * BLOCKS) * used
    source_all = picks.reshape(devices_all, devices_all, CAP).transpose(1, 0, 2)
    return (source_all.reshape(N_LAT, N_SLAB, N_LAT, N_SLAB, CAP), dest_all.reshape(N_LAT, N_SLAB, row_total))


def draw_source_row(key, part):
    return routes(key)[0]


def draw_dest_slot(key, part):
    return routes(key)[1]


def draw_diffusion_inverse(key, part):
    rows_ids = jnp.arange(LEV, dtype=jnp.int32)
    identity = jnp.where(rows_ids[:, None] == rows_ids[None, :], 1.0, 0.0).astype(jnp.float32)
    noise = jax.random.normal(key, (N_LAT, F, LEV, LEV), jnp.float32)
    return 0.9 * identity + noise * (0.5 / math.sqrt(LEV))


def block_levels(stream_key, dims, cuts, smallest, largest):
    loudness = 1.0
    for axis_at, parts in cuts:
        heights = jax.random.uniform(jax.random.fold_in(jax.random.fold_in(stream_key, 6), axis_at), (parts,), jnp.float32, smallest / len(cuts), largest / len(cuts))
        loudness = loudness * jnp.repeat(jnp.exp(heights), dims[axis_at] // parts).reshape((-1,) + (1,) * (len(dims) - 1 - axis_at))
    return loudness


def centred(key, shape, spread, most, pieces=(), kind=jnp.bfloat16):
    entries = spread * jax.random.normal(key, shape, jnp.float32)
    if pieces:
        entries = entries * block_levels(key, shape, pieces, -0.22, 0.18)
    return jnp.clip(entries, -most, most).astype(kind)


def setup_inputs(seed: int = 0) -> dict:
    key_list = jax.random.split(jax.random.key(seed), 7)
    field_state = centred(key_list[0], (N_LAT, LEV, BLOCKS, F, BW), 1.0, 6.0, ((0, 8), (1, 32)), jnp.float32)
    cotangent = centred(key_list[1], (N_LAT, LEV, BLOCKS, F, BW), 1.0, 6.0, ((0, 8), (2, 32)), jnp.float32)
    vertical_weight = jnp.clip(1.0 * jax.random.uniform(key_list[2], (N_LAT, LEV, BLOCKS, BW), jnp.float32) ** block_levels(key_list[2], (N_LAT, LEV, BLOCKS, BW), ((0, 8), (1, 32)), -0.2, 0.2), 0.0, 1.0)
    diffusion_inverse = draw_diffusion_inverse(jax.random.fold_in(key_list[6], 71), 0)
    source_row = draw_source_row(jax.random.fold_in(key_list[6], 71), 0)
    dest_slot = draw_dest_slot(jax.random.fold_in(key_list[6], 71), 0)
    return dict(field_state=field_state, cotangent=cotangent, vertical_weight=vertical_weight, diffusion_inverse=diffusion_inverse, source_row=source_row, dest_slot=dest_slot)


def reference(field_state, cotangent, vertical_weight, diffusion_inverse, source_row, dest_slot):
    highest = lax.Precision.HIGHEST
    devices_all = N_LAT * N_SLAB
    row_total = LEV_DEV * BLOCKS
    level_rows = field_state.reshape(devices_all * row_total, F, BW)
    weights = vertical_weight.reshape(devices_all, row_total, 1, BW)
    sender_first = source_row.reshape(devices_all, devices_all, CAP)
    slots = dest_slot.reshape(devices_all, row_total)
    sender = slots // CAP
    within = slots % CAP
    receiver = jnp.arange(devices_all, dtype=jnp.int32)[:, None]
    lower_idx = (sender * row_total + sender_first[sender, receiver, within]).astype(jnp.int32)
    upper_idx = (lower_idx + BLOCKS).astype(jnp.int32)
    lower_vals = level_rows[lower_idx]
    upper_vals = level_rows[upper_idx]
    moved = (1.0 - weights) * lower_vals + weights * upper_vals
    moved = moved.reshape(N_LAT, LEV, BLOCKS, F, BW)
    tangent_out = jnp.einsum('gflk,gkbfc->glbfc', diffusion_inverse, moved, precision=highest)
    back = jnp.einsum('gflk,glbfc->gkbfc', diffusion_inverse, cotangent, precision=highest)
    back = back.reshape(devices_all, row_total, F, BW)
    adjoint = jnp.zeros((devices_all * row_total, F, BW), jnp.float32)
    adjoint = adjoint.at[lower_idx.reshape(-1)].add(((1.0 - weights) * back).reshape(-1, F, BW))
    adjoint = adjoint.at[upper_idx.reshape(-1)].add((weights * back).reshape(-1, F, BW))
    return tangent_out, adjoint.reshape(N_LAT, LEV, BLOCKS, F, BW)
```

```python
import functools

import jax
import jax.numpy as jnp
from jax import lax
from jax.experimental import pallas as pl
from jax.experimental.pallas import tpu as pltpu
from jax.sharding import PartitionSpec as P

MESH = pl.DeviceIdType.MESH
VMEM_LIMIT = 56 << 20
F32 = jnp.float32
BF16 = jnp.bfloat16


def two_part_dot(table, values):
    high = values.astype(BF16)
    low = (values - high.astype(F32)).astype(BF16)
    return jnp.dot(table, high, preferred_element_type=F32) + jnp.dot(
        table, low, preferred_element_type=F32
    )


def one_hot(shape, ids, axis):
    return (lax.broadcasted_iota(jnp.int32, shape, axis) == ids).astype(F32).astype(BF16)


def columns_of(ref, f, fields, per, levels):
    parts = [ref[pl.ds(f * per + b, levels, stride=fields * per), :] for b in range(per)]
    return jnp.concatenate(parts, axis=1)


def start_kernel(fields, per, levels, slots, weights, cot, inverse, weight_out, back_out):
    table = one_hot((weight_out.shape[0], slots.shape[1]), slots[...], 0)
    weight_out[...] = two_part_dot(table, weights[...])
    for f in range(fields):
        out = lax.dot_general(
            inverse[f],
            columns_of(cot, f, fields, per, levels),
            (((0,), (0,)), ((), ())),
            precision=lax.Precision.HIGHEST,
            preferred_element_type=F32,
        )
        for b in range(per):
            back_out[pl.ds(f * per + b, levels, stride=fields * per), :] = out[:, b * 128 : (b + 1) * 128]


def spread_kernel(fields, slots, back, out):
    rows = slots.shape[1]
    table = one_hot((out.shape[1], rows), slots[...], 0)
    for f in range(fields):
        out[f] = two_part_dot(table, back[:, f].reshape(rows, 128))


def gather_kernel(fields, lower, weights, state, out):
    low_rows = 3 * 128
    table = one_hot((out.shape[1], low_rows), lower[...], 1)
    upper_part = weights[...]
    for f in range(fields):
        both = jnp.concatenate(
            [state[0:3, f].reshape(low_rows, 128), state[1:4, f].reshape(low_rows, 128)], axis=1
        )
        picked = two_part_dot(table, both)
        out[f] = (1.0 - upper_part) * picked[:, :128] + upper_part * picked[:, 128:]


def arrive_kernel(fields, slots, arrived, out):
    rows = slots.shape[0]
    table = one_hot((rows, arrived.shape[1]), slots[...], 1)
    for f in range(fields):
        out[:, f] = two_part_dot(table, arrived[f]).reshape(4, 128, 128)


def finish_kernel(fields, per, levels, moved, inverse, out):
    for f in range(fields):
        res = jnp.dot(
            inverse[f],
            columns_of(moved, f, fields, per, levels),
            precision=lax.Precision.HIGHEST,
            preferred_element_type=F32,
        )
        for b in range(per):
            out[pl.ds(f * per + b, levels, stride=fields * per), :] = res[:, b * 128 : (b + 1) * 128]


def scatter_kernel(fields, lower, weights, back, out):
    low_rows = 3 * 128
    table = one_hot((low_rows, lower.shape[1]), lower[...], 0)
    upper_part = weights[...]
    for f in range(fields):
        row = back[f]
        both = two_part_dot(
            table, jnp.concatenate([(1.0 - upper_part) * row, upper_part * row], axis=1)
        )
        low, high = both[:, :128].reshape(3, 128, 128), both[:, 128:].reshape(3, 128, 128)
        out[0, f] = low[0]
        out[1, f] = low[1] + high[0]
        out[2, f] = low[2] + high[1]
        out[3, f] = high[2]


def local(body, shapes, *args):
    return pl.pallas_call(
        body,
        out_shape=shapes,
        in_specs=[pl.BlockSpec(memory_space=pltpu.VMEM)] * len(args),
        out_specs=jax.tree.map(lambda _: pl.BlockSpec(memory_space=pltpu.VMEM), shapes),
        compiler_params=pltpu.CompilerParams(vmem_limit_bytes=VMEM_LIMIT),
    )(*args)


def shape(*dims):
    return jax.ShapeDtypeStruct(dims, F32)


def greet(g, s, n_lat, n_slab, lat, slab):
    bar = pltpu.get_barrier_semaphore()
    count = 0
    if lat:
        for k in range(1, n_lat):
            pl.semaphore_signal(bar, inc=1, device_id=((g + k) % n_lat, s), device_id_type=MESH)
        count += n_lat - 1
    if slab:

        def one(k, carry):
            pl.semaphore_signal(bar, inc=1, device_id=(g, (s + k) % n_slab), device_id_type=MESH)
            return carry

        lax.fori_loop(1, n_slab, one, 0)
        count += n_slab - 1
    pl.semaphore_wait(bar, count)


def slab_sends(g, s, n_slab, source, target, send, recv):
    pltpu.make_async_copy(source(s), target(s), recv).start()

    def one(k, carry):
        peer = (s + k) % n_slab
        pltpu.make_async_remote_copy(
            source(peer), target(s), send, recv, device_id=(g, peer), device_id_type=MESH
        ).start()
        return carry

    lax.fori_loop(1, n_slab, one, 0)


def lat_sends(g, s, n_lat, source, target, send, recv):
    pltpu.make_async_copy(source(g), target(g), recv).start()
    for k in (4, 1, 7, 2, 6, 3, 5):
        peer = (g + k) % n_lat
        pltpu.make_async_remote_copy(
            source(peer), target(g), send, recv, device_id=(peer, s), device_id_type=MESH
        ).start()


def wait_all(ref, sem):
    pltpu.make_async_copy(ref, ref, sem).wait()


def begin_comm(x, back, o, rows, xb, xs, xr, zs, zr, bs, br):
    g, s = lax.axis_index("lat"), lax.axis_index("slab")
    n_slab, n_lat = x.shape[0], x.shape[1]
    greet(g, s, n_lat, n_slab, True, True)
    slab_sends(g, s, n_slab, lambda p: x.at[p], lambda p: xb.at[p], xs, xr)
    slab_sends(g, s, n_slab, lambda p: back.at[p], lambda p: rows.at[:, :, p], bs, br)
    wait_all(xb, xr)
    lat_sends(g, s, n_lat, lambda p: xb.at[:, p], lambda p: o.at[p], zs, zr)
    wait_all(o, zr)
    wait_all(rows, br)
    wait_all(xb.at[: n_slab - 1], xs)
    wait_all(o.at[: n_lat - 1], zs)
    wait_all(back.at[: n_slab - 1], bs)


def forward_comm(x, o, zb, zs, zr, xs, xr):
    g, s = lax.axis_index("lat"), lax.axis_index("slab")
    fields, n_lat, n_slab = x.shape[:3]
    greet(g, s, n_lat, n_slab, True, True)
    for f in range(fields):
        lat_sends(g, s, n_lat, lambda p: x.at[f, p], lambda p: zb.at[f, p], zs.at[f], zr.at[f])
    for f in range(fields):
        wait_all(zb.at[f], zr.at[f])
        slab_sends(g, s, n_slab, lambda p: zb.at[f, :, p], lambda p: o.at[f, p], xs.at[f], xr.at[f])
    for f in range(fields):
        wait_all(o.at[f], xr.at[f])
        wait_all(x.at[f, : n_lat - 1], zs.at[f])
        wait_all(o.at[f, : n_slab - 1], xs.at[f])


def adjoint_comm(x, moved, o, levels, xb, xs, xr, zs, zr, ms, mr):
    g, s = lax.axis_index("lat"), lax.axis_index("slab")
    fields, n_slab, n_lat = x.shape[:3]
    greet(g, s, n_lat, n_slab, True, True)
    for f in range(fields):
        slab_sends(g, s, n_slab, lambda p: x.at[f, p], lambda p: xb.at[f, p], xs.at[f], xr.at[f])
    slab_sends(g, s, n_slab, lambda p: moved.at[:, :, p], lambda p: levels.at[p], ms, mr)
    for f in range(fields):
        wait_all(xb.at[f], xr.at[f])
        lat_sends(g, s, n_lat, lambda p: xb.at[f, :, p], lambda p: o.at[f, p], zs.at[f], zr.at[f])
    for f in range(fields):
        wait_all(o.at[f], zr.at[f])
        wait_all(o.at[f, : n_lat - 1], zs.at[f])
        wait_all(x.at[f, : n_slab - 1], xs.at[f])
    wait_all(levels, mr)
    wait_all(levels.at[: n_slab - 1], ms)


def comm(body, cid, shapes, scratch, *args):
    return pl.pallas_call(
        body,
        out_shape=shapes,
        in_specs=[pl.BlockSpec(memory_space=pl.ANY)] * len(args),
        out_specs=jax.tree.map(lambda _: pl.BlockSpec(memory_space=pl.ANY), shapes),
        scratch_shapes=scratch,
        compiler_params=pltpu.CompilerParams(
            vmem_limit_bytes=VMEM_LIMIT, collective_id=cid, has_side_effects=True
        ),
    )(*args)


def body(field_state, cotangent, vertical_weight, diffusion_inverse, source_row, dest_slot):
    _, here, blocks, fields, width = field_state.shape
    levels, per = cotangent.shape[1], cotangent.shape[2]
    n_lat, n_slab, cap = source_row.shape[2:]
    rows = here * blocks
    slot_total = n_lat * n_slab * cap
    dma = pltpu.SemaphoreType.DMA

    state = field_state.transpose(0, 1, 3, 2, 4).reshape(here, fields, blocks, width)
    cot = cotangent.transpose(0, 1, 3, 2, 4).reshape(levels * fields * per, width)
    weights = vertical_weight.reshape(rows, width)
    inverse = diffusion_inverse[0]
    lower = source_row.reshape(slot_total)
    slots = dest_slot.reshape(rows)
    sender, slot = slots // cap, slots % cap
    slots = ((sender % n_slab) * n_lat + sender // n_slab) * cap + slot
    slots_row, slots_col = slots.reshape(1, rows), slots.reshape(rows, 1)
    lower_row, lower_col = lower.reshape(1, slot_total), lower.reshape(slot_total, 1)

    weight_slots, back = local(
        functools.partial(start_kernel, fields, per, levels),
        (shape(slot_total, width), shape(levels * fields * per, width)),
        slots_row, weights, cot, inverse,
    )
    weight_own, back_rows = comm(
        begin_comm, 0,
        (shape(n_lat, n_slab, cap, width), shape(here, fields, n_slab, per, width)),
        [pltpu.VMEM((n_slab, n_lat, cap, width), F32)] + [dma] * 6,
        weight_slots.reshape(n_slab, n_lat, cap, width),
        back.reshape(n_slab, here, fields, per, width),
    )
    weight_own = weight_own.reshape(slot_total, width)
    sent = local(
        functools.partial(gather_kernel, fields), shape(fields, slot_total, width), lower_col, weight_own, state
    )
    arrived = comm(
        forward_comm, 1,
        shape(fields, n_slab, n_lat, cap, width),
        [pltpu.VMEM((fields, n_lat, n_slab, cap, width), F32)] + [dma((fields,))] * 4,
        sent.reshape(fields, n_lat, n_slab, cap, width),
    )
    moved = local(
        functools.partial(arrive_kernel, fields),
        shape(here, fields, blocks, width),
        slots_col, arrived.reshape(fields, slot_total, width),
    )
    spread = local(
        functools.partial(spread_kernel, fields),
        shape(fields, slot_total, width),
        slots_row, back_rows.reshape(here, fields, blocks, width),
    )
    returned, by_level = comm(
        adjoint_comm, 2,
        (shape(fields, n_lat, n_slab, cap, width), shape(n_slab, here, fields, per, width)),
        [pltpu.VMEM((fields, n_slab, n_lat, cap, width), F32)] + [dma((fields,))] * 4 + [dma] * 2,
        spread.reshape(fields, n_slab, n_lat, cap, width),
        moved.reshape(here, fields, n_slab, per, width),
    )
    tangent = local(
        functools.partial(finish_kernel, fields, per, levels),
        shape(levels * fields * per, width),
        by_level.reshape(levels * fields * per, width), inverse,
    )
    adjoint = local(
        functools.partial(scatter_kernel, fields),
        shape(here, fields, blocks, width),
        lower_row, weight_own, returned.reshape(fields, slot_total, width),
    )
    tangent = tangent.reshape(1, levels, fields, per, width).transpose(0, 1, 3, 2, 4)
    adjoint = adjoint.reshape(1, here, fields, blocks, width).transpose(0, 1, 3, 2, 4)
    return tangent, adjoint


def solution(mesh):
    placed = (
        P("lat", "slab", None, None, None),
        P("lat", None, "slab", None, None),
        P("lat", "slab", None, None),
        P("lat", None, None, None),
        P("lat", "slab", None, None, None),
        P("lat", "slab", None),
    )
    return jax.shard_map(
        body,
        mesh=mesh,
        in_specs=placed,
        out_specs=(P("lat", None, "slab", None, None), P("lat", "slab", None, None, None)),
        check_vma=False,
    )
```

```python
import functools

import jax
import jax.numpy as jnp
from jax import lax
from jax.experimental import pallas as pl
from jax.experimental.pallas import tpu as pltpu
from jax.sharding import PartitionSpec as P

MESH = pl.DeviceIdType.MESH
VMEM_LIMIT = 60 << 20
F32 = jnp.float32
BF16 = jnp.bfloat16


def split(values):
    high = values.astype(BF16)
    return high, (values - high.astype(F32)).astype(BF16)


def pick(table, values):
    width = values.shape[1]
    out = jnp.dot(table, jnp.concatenate(split(values), axis=1), preferred_element_type=F32)
    return out[:, :width] + out[:, width:]


def one_hot(shape, ids, axis):
    return (lax.broadcasted_iota(jnp.int32, shape, axis) == ids).astype(F32).astype(BF16)


def side_by_side(view, first, stride, per, levels):
    parts = [view[pl.ds(first + b, levels, stride=stride), :] for b in range(per)]
    return jnp.concatenate(parts, axis=1)


def lay_down(view, first, stride, per, levels, values):
    for b in range(per):
        view[pl.ds(first + b, levels, stride=stride), :] = values[:, b * 128 : (b + 1) * 128]


def signal_peers(g, s, n_lat, n_slab):
    bar = pltpu.get_barrier_semaphore()
    for k in range(1, n_lat):
        pl.semaphore_signal(bar, inc=1, device_id=((g + k) % n_lat, s), device_id_type=MESH)

    def one(k, carry):
        pl.semaphore_signal(bar, inc=1, device_id=(g, (s + k) % n_slab), device_id_type=MESH)
        return carry

    lax.fori_loop(1, n_slab, one, 0)


def wait_all(ref, sem):
    pltpu.make_async_copy(ref, ref, sem).wait()


def whole(
    slots_row, slots_col, lower_row, lower_col, weights, inverse, cot, state,
    tangent, adjoint,
    to_slot, from_slot, to_row, from_row,
    wx, wz, wo, bx, bk, fx, fz, fo, ax, ab, ao, mx, mo,
    w_sem, b_send, b_recv, fz_send, fz_recv, fx_send, fx_recv,
    az_send, az_recv, ax_send, ax_recv, m_send, m_recv,
):
    g, s = lax.axis_index("lat"), lax.axis_index("slab")
    fields, n_lat, n_slab, cap = fx.shape[:4]
    here, per = bk.shape[1], bk.shape[3]
    levels = n_slab * here
    blocks = n_slab * per
    slot_total = n_lat * n_slab * cap
    rows = here * blocks
    low_rows = rows - blocks

    def slab_sends(source, target, send, recv):
        pltpu.make_async_copy(source(s), target(s), recv).start()

        def one(k, carry):
            peer = (s + k) % n_slab
            pltpu.make_async_remote_copy(
                source(peer), target(s), send, recv, device_id=(g, peer), device_id_type=MESH
            ).start()
            return carry

        lax.fori_loop(1, n_slab, one, 0)

    def lat_sends(source, target, send, recv):
        pltpu.make_async_copy(source(g), target(g), recv).start()
        for k in (4, 1, 7, 2, 6, 3, 5):
            peer = (g + k) % n_lat
            pltpu.make_async_remote_copy(
                source(peer), target(g), send, recv, device_id=(peer, s), device_id_type=MESH
            ).start()

    def slot_rows(ref):
        return ref.reshape(fields * slot_total, 128)

    def local_rows(ref):
        return ref.reshape(fields * rows, 128)

    def at_field(f, count):
        return pl.ds(f * count, count)

    signal_peers(g, s, n_lat, n_slab)
    to_slot[...] = one_hot((slot_total, rows), slots_row[...], 0)
    wx.reshape(slot_total, 128)[...] = pick(to_slot[...], weights[...])
    pl.semaphore_wait(pltpu.get_barrier_semaphore(), n_lat + n_slab - 2)
    lat_sends(lambda p: wx.at[p], lambda p: wz.at[p], w_sem.at[0], w_sem.at[1])

    def backward(f):
        out = lax.dot_general(
            inverse[f],
            side_by_side(cot, f * per, fields * per, per, levels),
            (((0,), (0,)), ((), ())),
            precision=lax.Precision.HIGHEST,
            preferred_element_type=F32,
        )
        lay_down(local_rows(bx), f * rows, per, per, levels, out)
        slab_sends(lambda p: bx.at[f, p], lambda p: bk.at[f, :, p], b_send.at[f], b_recv.at[f])

    def spread(f):
        wait_all(bk.at[f], b_recv.at[f])
        slot_rows(ax)[at_field(f, slot_total), :] = pick(
            to_slot[...], local_rows(bk)[at_field(f, rows), :]
        )

    def gather(f):
        both = jnp.concatenate(
            [
                state[0 : here - 1, f].reshape(low_rows, 128),
                state[1:here, f].reshape(low_rows, 128),
            ],
            axis=1,
        )
        picked = pick(from_row[...], both)
        part = wo.reshape(slot_total, 128)[...]
        slot_rows(fx)[at_field(f, slot_total), :] = (1.0 - part) * picked[:, :128] + part * picked[:, 128:]
        lat_sends(lambda p: fx.at[f, p], lambda p: fz.at[f, p], fz_send.at[f], fz_recv.at[f])

    def pass_on(f):
        wait_all(fz.at[f], fz_recv.at[f])
        slab_sends(lambda p: fz.at[f, :, p], lambda p: fo.at[f, :, p], fx_send.at[f], fx_recv.at[f])

    def arrive(f):
        wait_all(fo.at[f], fx_recv.at[f])
        local_rows(mx)[at_field(f, rows), :] = pick(
            from_slot[...], slot_rows(fo)[at_field(f, slot_total), :]
        )
        slab_sends(lambda p: mx.at[f, :, p], lambda p: mo.at[f, p], m_send.at[f], m_recv.at[f])

    def finish(f):
        wait_all(mo.at[f], m_recv.at[f])
        out = jnp.dot(
            inverse[f],
            side_by_side(local_rows(mo), f * rows, per, per, levels),
            precision=lax.Precision.HIGHEST,
            preferred_element_type=F32,
        )
        lay_down(tangent, f * per, fields * per, per, levels, out)

    def adjoint_slab(f):
        slab_sends(lambda p: ax.at[f, :, p], lambda p: ab.at[f, :, p], ax_send.at[f], ax_recv.at[f])

    def adjoint_lat(f):
        wait_all(ab.at[f], ax_recv.at[f])
        lat_sends(lambda p: ab.at[f, p], lambda p: ao.at[f, p], az_send.at[f], az_recv.at[f])

    def scatter(f, sem):
        wait_all(ao.at[f], sem)
        row = slot_rows(ao)[at_field(f, slot_total), :]
        part = wo.reshape(slot_total, 128)[...]
        both = pick(to_row[...], jnp.concatenate([(1.0 - part) * row, part * row], axis=1))
        low = both[:, :128].reshape(here - 1, blocks, 128)
        high = both[:, 128:].reshape(here - 1, blocks, 128)
        adjoint[0, f] = low[0]
        for l in range(1, here - 1):
            adjoint[l, f] = low[l] + high[l - 1]
        adjoint[here - 1, f] = high[here - 2]

    for f in range(fields):
        backward(f)
    from_row[...] = one_hot((slot_total, low_rows), lower_col[...], 1)
    spread(0)
    lat_sends(lambda p: ax.at[0, p], lambda p: ab.at[0, p], az_send.at[0], az_recv.at[0])
    wait_all(wz, w_sem.at[1])
    slab_sends(lambda p: wz.at[:, p], lambda p: wo.at[:, p], w_sem.at[2], w_sem.at[3])
    spread(1)
    wait_all(wo, w_sem.at[3])
    for f in range(fields):
        gather(f)
    wait_all(ab.at[0], az_recv.at[0])
    slab_sends(lambda p: ab.at[0, :, p], lambda p: ao.at[0, :, p], ax_send.at[0], ax_recv.at[0])
    adjoint_slab(1)
    for f in range(2, fields):
        spread(f)
        adjoint_slab(f)
    from_slot[...] = one_hot((rows, slot_total), slots_col[...], 1)
    to_row[...] = one_hot((low_rows, slot_total), lower_row[...], 0)
    for f in range(fields):
        pass_on(f)
        if f == 0:
            scatter(0, ax_recv.at[0])
        if f >= 1:
            adjoint_lat(f)
            arrive(f - 1)
        if f >= 2:
            finish(f - 2)
    arrive(fields - 1)
    finish(fields - 2)
    finish(fields - 1)
    for f in range(1, fields):
        scatter(f, az_recv.at[f])

    wait_all(wz.at[: n_lat - 1], w_sem.at[0])
    wait_all(wo.at[:, : n_slab - 1], w_sem.at[2])
    for f in range(fields):
        wait_all(bx.at[f, : n_slab - 1], b_send.at[f])
        wait_all(fz.at[f, : n_lat - 1], fz_send.at[f])
        wait_all(fo.at[f, :, : n_slab - 1], fx_send.at[f])
        wait_all(mo.at[f, : n_slab - 1], m_send.at[f])
        wait_all(ao.at[f, : n_lat - 1], az_send.at[f])
        wait_all(ab.at[f, :, : n_slab - 1], ax_send.at[f])


def body(field_state, cotangent, vertical_weight, diffusion_inverse, source_row, dest_slot):
    _, here, blocks, fields, width = field_state.shape
    levels, per = cotangent.shape[1], cotangent.shape[2]
    n_lat, n_slab, cap = source_row.shape[2:]
    rows = here * blocks
    slot_total = n_lat * n_slab * cap
    low_rows = rows - blocks
    dma = pltpu.SemaphoreType.DMA

    state = field_state.transpose(0, 1, 3, 2, 4).reshape(here, fields, blocks, width)
    cot = cotangent.transpose(0, 1, 3, 2, 4).reshape(levels * fields * per, width)
    lower = source_row.reshape(slot_total)
    slots = dest_slot.reshape(rows)
    vmem = pl.BlockSpec(memory_space=pltpu.VMEM)
    slot_array = pltpu.VMEM((fields, n_lat, n_slab, cap, width), F32)
    weight_array = pltpu.VMEM((n_lat, n_slab, cap, width), F32)
    by_level = pltpu.VMEM((fields, here, n_slab, per, width), F32)
    by_block = pltpu.VMEM((fields, n_slab, here, per, width), F32)

    tangent, adjoint = pl.pallas_call(
        whole,
        out_shape=(
            jax.ShapeDtypeStruct((levels * fields * per, width), F32),
            jax.ShapeDtypeStruct((here, fields, blocks, width), F32),
        ),
        in_specs=[vmem] * 8,
        out_specs=(vmem, vmem),
        scratch_shapes=[
            pltpu.VMEM((slot_total, rows), BF16),
            pltpu.VMEM((rows, slot_total), BF16),
            pltpu.VMEM((low_rows, slot_total), BF16),
            pltpu.VMEM((slot_total, low_rows), BF16),
            weight_array, weight_array, weight_array,
            by_block, by_level,
            slot_array, slot_array, slot_array,
            slot_array, slot_array, slot_array,
            by_level, by_block,
            dma((4,)),
        ] + [dma((fields,))] * 12,
        compiler_params=pltpu.CompilerParams(
            vmem_limit_bytes=VMEM_LIMIT, collective_id=0, has_side_effects=True
        ),
    )(
        slots.reshape(1, rows), slots.reshape(rows, 1),
        lower.reshape(1, slot_total), lower.reshape(slot_total, 1),
        vertical_weight.reshape(rows, width), diffusion_inverse[0], cot, state,
    )
    tangent = tangent.reshape(1, levels, fields, per, width).transpose(0, 1, 3, 2, 4)
    adjoint = adjoint.reshape(1, here, fields, blocks, width).transpose(0, 1, 3, 2, 4)
    return tangent, adjoint


def solution(mesh):
    placed = (
        P("lat", "slab", None, None, None),
        P("lat", None, "slab", None, None),
        P("lat", "slab", None, None),
        P("lat", None, None, None),
        P("lat", "slab", None, None, None),
        P("lat", "slab", None),
    )
    return jax.shard_map(
        body,
        mesh=mesh,
        in_specs=placed,
        out_specs=(P("lat", None, "slab", None, None), P("lat", "slab", None, None, None)),
        check_vma=False,
    )
```

```python
import functools

import jax
import jax.numpy as jnp
from jax import lax
from jax.experimental import pallas as pl
from jax.experimental.pallas import tpu as pltpu
from jax.sharding import PartitionSpec as P

MESH = pl.DeviceIdType.MESH
VMEM_LIMIT = 60 << 20
F32 = jnp.float32
BF16 = jnp.bfloat16


def split(values):
    high = values.astype(BF16)
    return high, (values - high.astype(F32)).astype(BF16)


def pick(table, values):
    width = values.shape[1]
    out = jnp.dot(table, jnp.concatenate(split(values), axis=1), preferred_element_type=F32)
    return out[:, :width] + out[:, width:]


def iota(shape, axis):
    return lax.broadcasted_iota(jnp.int32, shape, axis)


def slab_peer(s, t):
    i = t + (t + 29) // 32
    q, j = i % 4, (i // 4) % 4
    dx = (q // 2) * (6 - 2 * q) + (1 - q // 2) * (1 + 2 * q)
    dy = dx + j + (j // 2) * (1 - 2 * (j % 2))
    x, y, core = s // 8, (s // 2) % 4, s % 2
    return ((x + dx) % 4) * 8 + ((y + dy) % 4) * 2 + (core + i // 16) % 2


def side_by_side(view, first, stride, per, levels):
    parts = [view[pl.ds(first + b, levels, stride=stride), :] for b in range(per)]
    return jnp.concatenate(parts, axis=1)


def lay_down(view, first, stride, per, levels, values):
    for b in range(per):
        view[pl.ds(first + b, levels, stride=stride), :] = values[:, b * 128 : (b + 1) * 128]


def signal_peers(g, s, n_lat, n_slab):
    bar = pltpu.get_barrier_semaphore()
    for k in range(1, n_lat):
        pl.semaphore_signal(bar, inc=1, device_id=((g + k) % n_lat, s), device_id_type=MESH)

    def one(k, carry):
        pl.semaphore_signal(bar, inc=1, device_id=(g, slab_peer(s, k)), device_id_type=MESH)
        return carry

    lax.fori_loop(0, n_slab - 1, one, 0)


def wait_all(ref, sem):
    pltpu.make_async_copy(ref, ref, sem).wait()


def whole(
    slots, lower, weights_in, inverse_in, cot_in, state_in,
    tangent_out, adjoint_out,
    weights, inverse, cot, state, tangent, adjoint,
    to_slot, from_slot, to_row, from_row,
    wx, wz, wo, bx, bk, fx, fz, fo, ax, ab, ao, mx, mo,
    w_sem, b_send, b_recv, fz_send, fz_recv, fx_send, fx_recv,
    az_send, az_recv, ax_send, ax_recv, m_send, m_recv,
    in_sem, out_sem,
):
    g, s = lax.axis_index("lat"), lax.axis_index("slab")
    fields, n_lat, n_slab, cap = fx.shape[:4]
    here, per = bk.shape[1], bk.shape[3]
    levels = n_slab * here
    blocks = n_slab * per
    slot_total = n_lat * n_slab * cap
    rows = here * blocks
    low_rows = rows - blocks

    def slab_sends(source, target, send, recv):
        pltpu.make_async_copy(source(s), target(s), recv).start()

        def one(k, carry):
            peer = slab_peer(s, k)
            pltpu.make_async_remote_copy(
                source(peer), target(s), send, recv, device_id=(g, peer), device_id_type=MESH
            ).start()
            return carry

        lax.fori_loop(0, n_slab - 1, one, 0)

    def lat_sends(source, target, send, recv):
        pltpu.make_async_copy(source(g), target(g), recv).start()
        for k in (4, 1, 7, 2, 6, 3, 5):
            peer = (g + k) % n_lat
            pltpu.make_async_remote_copy(
                source(peer), target(g), send, recv, device_id=(peer, s), device_id_type=MESH
            ).start()

    def slot_rows(ref):
        return ref.reshape(fields * slot_total, 128)

    def local_rows(ref):
        return ref.reshape(fields * rows, 128)

    def at_field(f, count):
        return pl.ds(f * count, count)

    inputs = [
        pltpu.make_async_copy(a, b, in_sem.at[i])
        for i, (a, b) in enumerate(
            [(weights_in, weights), (inverse_in, inverse), (cot_in, cot), (state_in, state)]
        )
    ]
    for copy in inputs:
        copy.start()
    signal_peers(g, s, n_lat, n_slab)
    to_slot[...] = (iota((slot_total, rows), 0) == slots[...]).astype(F32).astype(BF16)
    inputs[0].wait()
    wx.reshape(slot_total, 128)[...] = pick(to_slot[...], weights[...])
    pl.semaphore_wait(pltpu.get_barrier_semaphore(), n_lat + n_slab - 2)
    lat_sends(lambda p: wx.at[p], lambda p: wz.at[p], w_sem.at[0], w_sem.at[1])

    def backward(f):
        out = lax.dot_general(
            inverse[f],
            side_by_side(cot, f * per, fields * per, per, levels),
            (((0,), (0,)), ((), ())),
            precision=lax.Precision.HIGHEST,
            preferred_element_type=F32,
        )
        lay_down(local_rows(bx), f * rows, per, per, levels, out)

    def backward_slab(f):
        slab_sends(lambda p: bx.at[f, p], lambda p: bk.at[f, :, p], b_send.at[f], b_recv.at[f])

    def spread(f):
        wait_all(bk.at[f], b_recv.at[f])
        slot_rows(ax)[at_field(f, slot_total), :] = pick(
            to_slot[...], local_rows(bk)[at_field(f, rows), :]
        )

    def gather(f):
        both = jnp.concatenate(
            [
                state[0 : here - 1, f].reshape(low_rows, 128),
                state[1:here, f].reshape(low_rows, 128),
            ],
            axis=1,
        )
        picked = pick(from_row[...], both)
        part = wo.reshape(slot_total, 128)[...]
        slot_rows(fx)[at_field(f, slot_total), :] = (1.0 - part) * picked[:, :128] + part * picked[:, 128:]
        lat_sends(lambda p: fx.at[f, p], lambda p: fz.at[f, p], fz_send.at[f], fz_recv.at[f])

    def pass_on(f):
        wait_all(fz.at[f], fz_recv.at[f])
        slab_sends(lambda p: fz.at[f, :, p], lambda p: fo.at[f, :, p], fx_send.at[f], fx_recv.at[f])

    def arrive(f):
        wait_all(fo.at[f], fx_recv.at[f])
        local_rows(mx)[at_field(f, rows), :] = pick(
            from_slot[...], slot_rows(fo)[at_field(f, slot_total), :]
        )
        slab_sends(lambda p: mx.at[f, :, p], lambda p: mo.at[f, p], m_send.at[f], m_recv.at[f])

    def finish(f):
        wait_all(mo.at[f], m_recv.at[f])
        out = jnp.dot(
            inverse[f],
            side_by_side(local_rows(mo), f * rows, per, per, levels),
            precision=lax.Precision.HIGHEST,
            preferred_element_type=F32,
        )
        lay_down(tangent, f * per, fields * per, per, levels, out)

    def adjoint_slab(f):
        slab_sends(lambda p: ax.at[f, :, p], lambda p: ab.at[f, :, p], ax_send.at[f], ax_recv.at[f])

    def adjoint_lat(f):
        wait_all(ab.at[f], ax_recv.at[f])
        lat_sends(lambda p: ab.at[f, p], lambda p: ao.at[f, p], az_send.at[f], az_recv.at[f])

    def scatter(f, sem):
        wait_all(ao.at[f], sem)
        row = slot_rows(ao)[at_field(f, slot_total), :]
        part = wo.reshape(slot_total, 128)[...]
        both = pick(to_row[...], jnp.concatenate([(1.0 - part) * row, part * row], axis=1))
        low = both[:, :128].reshape(here - 1, blocks, 128)
        high = both[:, 128:].reshape(here - 1, blocks, 128)
        adjoint[0, f] = low[0]
        for l in range(1, here - 1):
            adjoint[l, f] = low[l] + high[l - 1]
        adjoint[here - 1, f] = high[here - 2]
        pltpu.make_async_copy(adjoint.at[:, f], adjoint_out.at[:, f], out_sem.at[f]).start()

    each = n_slab * cap

    def row_table(p):
        widen = (iota((each, n_slab), 0) // cap == iota((each, n_slab), 1)).astype(F32)
        by_slot = lax.dot_general(
            widen,
            lower[p].astype(F32),
            (((1,), (1,)), ((), ())),
            precision=lax.Precision.HIGHEST,
            preferred_element_type=F32,
        )
        here_only = iota((each, cap), 0) % cap == iota((each, cap), 1)
        ids = jnp.sum(jnp.where(here_only, by_slot, 0.0), axis=1, keepdims=True).astype(jnp.int32)
        return (iota((each, low_rows), 1) == ids).astype(F32)

    inputs[1].wait()
    inputs[2].wait()
    backward(0)
    backward_slab(0)
    for p in range(n_lat):
        from_row[p * each : (p + 1) * each, :] = row_table(p).astype(BF16)
    spread(0)
    for f in range(1, fields):
        backward(f)
    inputs[3].wait()
    wait_all(wz, w_sem.at[1])
    lat_sends(lambda p: ax.at[0, p], lambda p: ab.at[0, p], az_send.at[0], az_recv.at[0])
    slab_sends(lambda p: wz.at[:, p], lambda p: wo.at[:, p], w_sem.at[2], w_sem.at[3])
    for f in range(1, fields):
        backward_slab(f)
    wait_all(wo, w_sem.at[3])
    for f in range(fields):
        gather(f)
    spread(1)
    adjoint_slab(1)
    wait_all(ab.at[0], az_recv.at[0])
    slab_sends(lambda p: ab.at[0, :, p], lambda p: ao.at[0, :, p], ax_send.at[0], ax_recv.at[0])
    for f in range(2, fields):
        spread(f)
        adjoint_slab(f)
    for p in range(n_lat):
        ids = iota((each, rows), 0) + p * each
        from_slot[:, p * each : (p + 1) * each] = (ids == slots[...]).astype(F32).T.astype(BF16)
        to_row[:, p * each : (p + 1) * each] = row_table(p).T.astype(BF16)
    for f in range(fields):
        pass_on(f)
        if f == 3:
            scatter(0, ax_recv.at[0])
        if f < 2:
            adjoint_lat(2 * f + 1)
            adjoint_lat(2 * f + 2)
        if f >= 1:
            arrive(f - 1)
        if f >= 2:
            finish(f - 2)
    arrive(fields - 1)
    finish(fields - 2)
    finish(fields - 1)
    tangent_copy = pltpu.make_async_copy(tangent, tangent_out, out_sem.at[fields])
    tangent_copy.start()
    for f in range(1, fields):
        scatter(f, az_recv.at[f])

    wait_all(wz.at[: n_lat - 1], w_sem.at[0])
    wait_all(wo.at[:, : n_slab - 1], w_sem.at[2])
    for f in range(fields):
        wait_all(bx.at[f, : n_slab - 1], b_send.at[f])
        wait_all(fz.at[f, : n_lat - 1], fz_send.at[f])
        wait_all(fo.at[f, :, : n_slab - 1], fx_send.at[f])
        wait_all(mo.at[f, : n_slab - 1], m_send.at[f])
        wait_all(ao.at[f, : n_lat - 1], az_send.at[f])
        wait_all(ab.at[f, :, : n_slab - 1], ax_send.at[f])
    tangent_copy.wait()
    for f in range(fields):
        pltpu.make_async_copy(adjoint.at[:, f], adjoint_out.at[:, f], out_sem.at[f]).wait()


def settle(first_in, second_in, first_out, second_out, sems):
    copies = []
    for i, (a, b) in enumerate(((first_in, first_out), (second_in, second_out))):
        for j in range(4):
            part = a.shape[0] // 4
            cut = pl.ds(j * part, part)
            copies.append(pltpu.make_async_copy(a.at[cut], b.at[cut], sems.at[4 * i + j]))
    for copy in copies:
        copy.start()
    for copy in copies:
        copy.wait()


def body(field_state, cotangent, vertical_weight, diffusion_inverse, source_row, dest_slot):
    _, here, blocks, fields, width = field_state.shape
    levels, per = cotangent.shape[1], cotangent.shape[2]
    n_lat, n_slab, cap = source_row.shape[2:]
    rows = here * blocks
    slot_total = n_lat * n_slab * cap
    low_rows = rows - blocks
    dma = pltpu.SemaphoreType.DMA

    state = field_state.transpose(0, 1, 3, 2, 4).reshape(here, fields, blocks, width)
    cot = cotangent.transpose(0, 1, 3, 2, 4).reshape(levels * fields * per, width)
    lower = source_row.reshape(n_lat, n_slab, cap).transpose(0, 2, 1)
    vmem = pl.BlockSpec(memory_space=pltpu.VMEM)
    anywhere = pl.BlockSpec(memory_space=pl.ANY)
    slot_array = pltpu.VMEM((fields, n_lat, n_slab, cap, width), F32)
    weight_array = pltpu.VMEM((n_lat, n_slab, cap, width), F32)
    by_level = pltpu.VMEM((fields, here, n_slab, per, width), F32)
    by_block = pltpu.VMEM((fields, n_slab, here, per, width), F32)

    shapes = (
        jax.ShapeDtypeStruct((levels * fields * per, width), F32),
        jax.ShapeDtypeStruct((here, fields, blocks, width), F32),
    )
    results = pl.pallas_call(
        whole,
        out_shape=shapes,
        in_specs=[vmem] * 2 + [anywhere] * 4,
        out_specs=(anywhere, anywhere),
        scratch_shapes=[
            pltpu.VMEM((rows, width), F32),
            pltpu.VMEM((fields, levels, levels), F32),
            pltpu.VMEM((levels * fields * per, width), F32),
            pltpu.VMEM((here, fields, blocks, width), F32),
            pltpu.VMEM((levels * fields * per, width), F32),
            pltpu.VMEM((here, fields, blocks, width), F32),
            pltpu.VMEM((slot_total, rows), BF16),
            pltpu.VMEM((rows, slot_total), BF16),
            pltpu.VMEM((low_rows, slot_total), BF16),
            pltpu.VMEM((slot_total, low_rows), BF16),
            weight_array, weight_array, weight_array,
            by_block, by_level,
            slot_array, slot_array, slot_array,
            slot_array, slot_array, slot_array,
            by_level, by_block,
            dma((4,)),
        ] + [dma((fields,))] * 12 + [dma((4,)), dma((fields + 1,))],
        compiler_params=pltpu.CompilerParams(
            vmem_limit_bytes=VMEM_LIMIT, collective_id=0, has_side_effects=True
        ),
    )(
        dest_slot.reshape(1, rows), lower,
        vertical_weight.reshape(rows, width), diffusion_inverse[0], cot, state,
    )
    tangent, adjoint = results
    tangent = tangent.reshape(1, levels, fields, per, width).transpose(0, 1, 3, 2, 4)
    adjoint = adjoint.reshape(1, here, fields, blocks, width).transpose(0, 1, 3, 2, 4)
    return tangent, adjoint


def solution(mesh):
    placed = (
        P("lat", "slab", None, None, None),
        P("lat", None, "slab", None, None),
        P("lat", "slab", None, None),
        P("lat", None, None, None),
        P("lat", "slab", None, None, None),
        P("lat", "slab", None),
    )
    return jax.shard_map(
        body,
        mesh=mesh,
        in_specs=placed,
        out_specs=(P("lat", None, "slab", None, None), P("lat", "slab", None, None, None)),
        check_vma=False,
    )
```

```python
import functools

import jax
import jax.numpy as jnp
from jax import lax
from jax.experimental import pallas as pl
from jax.experimental.pallas import tpu as pltpu
from jax.sharding import PartitionSpec as P

MESH = pl.DeviceIdType.MESH
VMEM_LIMIT = 60 << 20
F32 = jnp.float32
BF16 = jnp.bfloat16


def split(values):
    high = values.astype(BF16)
    return high, (values - high.astype(F32)).astype(BF16)


def pick(table, values):
    width = values.shape[1]
    out = jnp.dot(table, jnp.concatenate(split(values), axis=1), preferred_element_type=F32)
    return out[:, :width] + out[:, width:]


def iota(shape, axis):
    return lax.broadcasted_iota(jnp.int32, shape, axis)


def slab_peer(s, t):
    i = t + (t + 29) // 32
    q, j = i % 4, (i // 4) % 4
    dx = (q // 2) * (6 - 2 * q) + (1 - q // 2) * (1 + 2 * q)
    dy = dx + j + (j // 2) * (1 - 2 * (j % 2))
    x, y, core = s // 8, (s // 2) % 4, s % 2
    return ((x + dx) % 4) * 8 + ((y + dy) % 4) * 2 + (core + i // 16) % 2


def side_by_side(view, first, stride, per, levels):
    parts = [view[pl.ds(first + b, levels, stride=stride), :] for b in range(per)]
    return jnp.concatenate(parts, axis=1)


def lay_down(view, first, stride, per, levels, values):
    for b in range(per):
        view[pl.ds(first + b, levels, stride=stride), :] = values[:, b * 128 : (b + 1) * 128]


def signal_peers(g, s, n_lat, n_slab):
    bar = pltpu.get_barrier_semaphore()
    for k in range(1, n_lat):
        pl.semaphore_signal(bar, inc=1, device_id=((g + k) % n_lat, s), device_id_type=MESH)

    def one(k, carry):
        pl.semaphore_signal(bar, inc=1, device_id=(g, slab_peer(s, k)), device_id_type=MESH)
        return carry

    lax.fori_loop(0, n_slab - 1, one, 0)


def wait_all(ref, sem):
    pltpu.make_async_copy(ref, ref, sem).wait()


def whole(
    slots, lower, weights_in, inverse_in, cot_in, state_in,
    tangent_out, adjoint_out,
    weights, inverse, cot, state, tangent, adjoint,
    to_slot, from_slot, to_row, from_row,
    wx, wz, wo, bx, bk, fx, fz, fo, ax, ab, ao, mx, mo,
    w_sem, b_send, b_recv, fz_send, fz_recv, fx_send, fx_recv,
    az_send, az_recv, ax_send, ax_recv, m_send, m_recv,
    in_sem, out_sem, last_recv,
):
    g, s = lax.axis_index("lat"), lax.axis_index("slab")
    fields, n_lat, n_slab, cap = fx.shape[:4]
    here, per = bk.shape[1], bk.shape[3]
    levels = n_slab * here
    blocks = n_slab * per
    slot_total = n_lat * n_slab * cap
    rows = here * blocks
    low_rows = rows - blocks

    def slab_sends(source, target, send, recv):
        pltpu.make_async_copy(source(s), target(s), recv).start()

        def one(k, carry):
            peer = slab_peer(s, k)
            pltpu.make_async_remote_copy(
                source(peer), target(s), send, recv, device_id=(g, peer), device_id_type=MESH
            ).start()
            return carry

        lax.fori_loop(0, n_slab - 1, one, 0)

    def lat_sends(source, target, send, recv):
        pltpu.make_async_copy(source(g), target(g), recv).start()
        for k in (4, 1, 7, 2, 6, 3, 5):
            peer = (g + k) % n_lat
            pltpu.make_async_remote_copy(
                source(peer), target(g), send, recv, device_id=(peer, s), device_id_type=MESH
            ).start()

    def slot_rows(ref):
        return ref.reshape(fields * slot_total, 128)

    def local_rows(ref):
        return ref.reshape(fields * rows, 128)

    def at_field(f, count):
        return pl.ds(f * count, count)

    inputs = [
        pltpu.make_async_copy(a, b, in_sem.at[i])
        for i, (a, b) in enumerate(
            [(weights_in, weights), (inverse_in, inverse), (cot_in, cot), (state_in, state)]
        )
    ]
    inputs[0].start()
    signal_peers(g, s, n_lat, n_slab)
    for copy in inputs[1:]:
        copy.start()
    each = n_slab * cap
    inputs[0].wait()
    weight_parts = jnp.concatenate(split(weights[...]), axis=1)
    for k in (4, 1, 7, 2, 6, 3, 5, 0):
        p = (g + k) % n_lat
        here_rows = pl.ds(pl.multiple_of(p * each, each), each)
        table = (iota((each, rows), 0) + p * each == slots[...]).astype(F32).astype(BF16)
        to_slot[here_rows, :] = table
        out = jnp.dot(table, weight_parts, preferred_element_type=F32)
        wx.reshape(slot_total, 128)[here_rows, :] = out[:, :128] + out[:, 128:]
        if k == 4:
            pl.semaphore_wait(pltpu.get_barrier_semaphore(), n_lat + n_slab - 2)
        if k == 0:
            pltpu.make_async_copy(wx.at[p], wz.at[p], w_sem.at[1]).start()
        else:
            pltpu.make_async_remote_copy(
                wx.at[p], wz.at[g], w_sem.at[0], w_sem.at[1], device_id=(p, s), device_id_type=MESH
            ).start()

    def backward(f):
        out = lax.dot_general(
            inverse[f],
            side_by_side(cot, f * per, fields * per, per, levels),
            (((0,), (0,)), ((), ())),
            precision=lax.Precision.HIGHEST,
            preferred_element_type=F32,
        )
        lay_down(local_rows(bx), f * rows, per, per, levels, out)

    def backward_slab(f):
        slab_sends(lambda p: bx.at[f, p], lambda p: bk.at[f, :, p], b_send.at[f], b_recv.at[f])

    def spread(f):
        wait_all(bk.at[f], b_recv.at[f])
        slot_rows(ax)[at_field(f, slot_total), :] = pick(
            to_slot[...], local_rows(bk)[at_field(f, rows), :]
        )

    def gather(f):
        both = jnp.concatenate(
            [
                state[0 : here - 1, f].reshape(low_rows, 128),
                state[1:here, f].reshape(low_rows, 128),
            ],
            axis=1,
        )
        picked = pick(from_row[...], both)
        part = wo.reshape(slot_total, 128)[...]
        slot_rows(fx)[at_field(f, slot_total), :] = (1.0 - part) * picked[:, :128] + part * picked[:, 128:]
        lat_sends(lambda p: fx.at[f, p], lambda p: fz.at[f, p], fz_send.at[f], fz_recv.at[f])

    def pass_on(f):
        wait_all(fz.at[f], fz_recv.at[f])
        slab_sends(lambda p: fz.at[f, :, p], lambda p: fo.at[f, :, p], fx_send.at[f], fx_recv.at[f])

    def arrive(f):
        wait_all(fo.at[f], fx_recv.at[f])
        local_rows(mx)[at_field(f, rows), :] = pick(
            from_slot[...], slot_rows(fo)[at_field(f, slot_total), :]
        )
        slab_sends(lambda p: mx.at[f, :, p], lambda p: mo.at[f, p], m_send.at[f], m_recv.at[f])

    def finish(f):
        wait_all(mo.at[f], m_recv.at[f])
        out = jnp.dot(
            inverse[f],
            side_by_side(local_rows(mo), f * rows, per, per, levels),
            precision=lax.Precision.HIGHEST,
            preferred_element_type=F32,
        )
        lay_down(tangent, f * per, fields * per, per, levels, out)

    def adjoint_slab(f):
        slab_sends(lambda p: ax.at[f, :, p], lambda p: ab.at[f, :, p], ax_send.at[f], ax_recv.at[f])

    def adjoint_lat(f):
        wait_all(ab.at[f], ax_recv.at[f])
        recv = last_recv.at[g] if f == fields - 1 else az_recv.at[f]
        lat_sends(lambda p: ab.at[f, p], lambda p: ao.at[f, p], az_send.at[f], recv)

    def contributions(table, row, part):
        return pick(table, jnp.concatenate([(1.0 - part) * row, part * row], axis=1))

    def scatter(f, sem):
        wait_all(ao.at[f], sem)
        row = slot_rows(ao)[at_field(f, slot_total), :]
        put(f, contributions(to_row[...], row, wo.reshape(slot_total, 128)[...]))

    def scatter_last(f):
        both = jnp.zeros((low_rows, 256), F32)
        for k in (0, 1, 7, 2, 6, 3, 5, 4):
            p = (g + k) % n_lat
            wait_all(ao.at[f, p], last_recv.at[p])
            first = pl.multiple_of(p * each, each)
            both += contributions(
                to_row[:, pl.ds(first, each)],
                slot_rows(ao)[pl.ds(f * slot_total + first, each), :],
                wo.reshape(slot_total, 128)[pl.ds(first, each), :],
            )
        put(f, both)

    def put(f, both):
        low = both[:, :128].reshape(here - 1, blocks, 128)
        high = both[:, 128:].reshape(here - 1, blocks, 128)
        adjoint[0, f] = low[0]
        for l in range(1, here - 1):
            adjoint[l, f] = low[l] + high[l - 1]
        adjoint[here - 1, f] = high[here - 2]
        pltpu.make_async_copy(adjoint.at[:, f], adjoint_out.at[:, f], out_sem.at[f]).start()

    def row_table(p):
        widen = (iota((each, n_slab), 0) // cap == iota((each, n_slab), 1)).astype(F32)
        by_slot = lax.dot_general(
            widen,
            lower[p].astype(F32),
            (((1,), (1,)), ((), ())),
            precision=lax.Precision.HIGHEST,
            preferred_element_type=F32,
        )
        here_only = iota((each, cap), 0) % cap == iota((each, cap), 1)
        ids = jnp.sum(jnp.where(here_only, by_slot, 0.0), axis=1, keepdims=True).astype(jnp.int32)
        return (iota((each, low_rows), 1) == ids).astype(F32)

    early = 2

    def early_lat(f):
        lat_sends(lambda p: ax.at[f, p], lambda p: ab.at[f, p], az_send.at[f], az_recv.at[f])

    def early_slab(f):
        wait_all(ab.at[f], az_recv.at[f])
        slab_sends(lambda p: ab.at[f, :, p], lambda p: ao.at[f, :, p], ax_send.at[f], ax_recv.at[f])

    inputs[1].wait()
    inputs[2].wait()
    for f in range(early):
        backward(f)
        backward_slab(f)
    for p in range(n_lat):
        from_row[p * each : (p + 1) * each, :] = row_table(p).astype(BF16)
    spread(0)
    early_lat(0)
    for f in range(1, early):
        spread(f)
    for f in range(early, fields):
        backward(f)
    inputs[3].wait()
    wait_all(wz, w_sem.at[1])
    slab_sends(lambda p: wz.at[:, p], lambda p: wo.at[:, p], w_sem.at[2], w_sem.at[3])
    for f in range(1, early):
        early_lat(f)
    for f in range(early, fields):
        backward_slab(f)
    wait_all(wo, w_sem.at[3])
    for f in range(fields):
        gather(f)
    early_slab(0)
    for f in range(early, fields):
        spread(f)
        adjoint_slab(f)
    for f in range(1, early):
        early_slab(f)
    for p in range(n_lat):
        ids = iota((each, rows), 0) + p * each
        from_slot[:, p * each : (p + 1) * each] = (ids == slots[...]).astype(F32).T.astype(BF16)
        to_row[:, p * each : (p + 1) * each] = row_table(p).T.astype(BF16)
    for f in range(fields):
        pass_on(f)
        if f < fields - early:
            adjoint_lat(early + f)
        if f >= 1:
            arrive(f - 1)
        if f >= 2:
            finish(f - 2)
        if f >= fields - early:
            scatter(f - fields + early, ax_recv.at[f - fields + early])
    arrive(fields - 1)
    finish(fields - 2)
    finish(fields - 1)
    tangent_copy = pltpu.make_async_copy(tangent, tangent_out, out_sem.at[fields])
    tangent_copy.start()
    for f in range(early, fields - 1):
        scatter(f, az_recv.at[f])
    scatter_last(fields - 1)

    wait_all(wz.at[: n_lat - 1], w_sem.at[0])
    wait_all(wo.at[:, : n_slab - 1], w_sem.at[2])
    for f in range(fields):
        wait_all(bx.at[f, : n_slab - 1], b_send.at[f])
        wait_all(fz.at[f, : n_lat - 1], fz_send.at[f])
        wait_all(fo.at[f, :, : n_slab - 1], fx_send.at[f])
        wait_all(mo.at[f, : n_slab - 1], m_send.at[f])
        wait_all(ao.at[f, : n_lat - 1], az_send.at[f])
        wait_all(ab.at[f, :, : n_slab - 1], ax_send.at[f])
    tangent_copy.wait()
    for f in range(fields):
        pltpu.make_async_copy(adjoint.at[:, f], adjoint_out.at[:, f], out_sem.at[f]).wait()


def body(field_state, cotangent, vertical_weight, diffusion_inverse, source_row, dest_slot):
    _, here, blocks, fields, width = field_state.shape
    levels, per = cotangent.shape[1], cotangent.shape[2]
    n_lat, n_slab, cap = source_row.shape[2:]
    rows = here * blocks
    slot_total = n_lat * n_slab * cap
    low_rows = rows - blocks
    dma = pltpu.SemaphoreType.DMA

    state = field_state.transpose(0, 1, 3, 2, 4).reshape(here, fields, blocks, width)
    cot = cotangent.transpose(0, 1, 3, 2, 4).reshape(levels * fields * per, width)
    lower = source_row.reshape(n_lat, n_slab, cap).transpose(0, 2, 1)
    vmem = pl.BlockSpec(memory_space=pltpu.VMEM)
    anywhere = pl.BlockSpec(memory_space=pl.ANY)
    slot_array = pltpu.VMEM((fields, n_lat, n_slab, cap, width), F32)
    weight_array = pltpu.VMEM((n_lat, n_slab, cap, width), F32)
    by_level = pltpu.VMEM((fields, here, n_slab, per, width), F32)
    by_block = pltpu.VMEM((fields, n_slab, here, per, width), F32)

    shapes = (
        jax.ShapeDtypeStruct((levels * fields * per, width), F32),
        jax.ShapeDtypeStruct((here, fields, blocks, width), F32),
    )
    results = pl.pallas_call(
        whole,
        out_shape=shapes,
        in_specs=[vmem] * 2 + [anywhere] * 4,
        out_specs=(anywhere, anywhere),
        scratch_shapes=[
            pltpu.VMEM((rows, width), F32),
            pltpu.VMEM((fields, levels, levels), F32),
            pltpu.VMEM((levels * fields * per, width), F32),
            pltpu.VMEM((here, fields, blocks, width), F32),
            pltpu.VMEM((levels * fields * per, width), F32),
            pltpu.VMEM((here, fields, blocks, width), F32),
            pltpu.VMEM((slot_total, rows), BF16),
            pltpu.VMEM((rows, slot_total), BF16),
            pltpu.VMEM((low_rows, slot_total), BF16),
            pltpu.VMEM((slot_total, low_rows), BF16),
            weight_array, weight_array, weight_array,
            by_block, by_level,
            slot_array, slot_array, slot_array,
            slot_array, slot_array, slot_array,
            by_level, by_block,
            dma((4,)),
        ] + [dma((fields,))] * 12 + [dma((4,)), dma((fields + 1,)), dma((n_lat,))],
        compiler_params=pltpu.CompilerParams(
            vmem_limit_bytes=VMEM_LIMIT, collective_id=0, has_side_effects=True
        ),
    )(
        dest_slot.reshape(1, rows), lower,
        vertical_weight.reshape(rows, width), diffusion_inverse[0], cot, state,
    )
    tangent, adjoint = results
    tangent = tangent.reshape(1, levels, fields, per, width).transpose(0, 1, 3, 2, 4)
    adjoint = adjoint.reshape(1, here, fields, blocks, width).transpose(0, 1, 3, 2, 4)
    return tangent, adjoint


def solution(mesh):
    placed = (
        P("lat", "slab", None, None, None),
        P("lat", None, "slab", None, None),
        P("lat", "slab", None, None),
        P("lat", None, None, None),
        P("lat", "slab", None, None, None),
        P("lat", "slab", None),
    )
    return jax.shard_map(
        body,
        mesh=mesh,
        in_specs=placed,
        out_specs=(P("lat", None, "slab", None, None), P("lat", "slab", None, None, None)),
        check_vma=False,
    )
```

```python
import functools

import jax
import jax.numpy as jnp
from jax import lax
from jax.experimental import pallas as pl
from jax.experimental.pallas import tpu as pltpu
from jax.sharding import PartitionSpec as P

MESH = pl.DeviceIdType.MESH
VMEM_LIMIT = 40 << 20
F32 = jnp.float32
BF16 = jnp.bfloat16


def split(values):
    high = values.astype(BF16)
    return high, (values - high.astype(F32)).astype(BF16)


def pick(table, values):
    width = values.shape[1]
    out = jnp.dot(table, jnp.concatenate(split(values), axis=1), preferred_element_type=F32)
    return out[:, :width] + out[:, width:]


def iota(shape, axis):
    return lax.broadcasted_iota(jnp.int32, shape, axis)


def slab_peer(s, t):
    i = t + (t + 29) // 32
    q, j = i % 4, (i // 4) % 4
    dx = (q // 2) * (6 - 2 * q) + (1 - q // 2) * (1 + 2 * q)
    dy = dx + j + (j // 2) * (1 - 2 * (j % 2))
    x, y, core = s // 8, (s // 2) % 4, s % 2
    return ((x + dx) % 4) * 8 + ((y + dy) % 4) * 2 + (core + i // 16) % 2


def side_by_side(view, first, stride, per, levels):
    parts = [view[pl.ds(first + b, levels, stride=stride), :] for b in range(per)]
    return jnp.concatenate(parts, axis=1)


def lay_down(view, first, stride, per, levels, values):
    for b in range(per):
        view[pl.ds(first + b, levels, stride=stride), :] = values[:, b * 128 : (b + 1) * 128]


def signal_peers(g, s, n_lat, n_slab):
    bar = pltpu.get_barrier_semaphore()
    for k in range(1, n_lat):
        pl.semaphore_signal(bar, inc=1, device_id=((g + k) % n_lat, s), device_id_type=MESH)

    def one(k, carry):
        pl.semaphore_signal(bar, inc=1, device_id=(g, slab_peer(s, k)), device_id_type=MESH)
        return carry

    lax.fori_loop(0, n_slab - 1, one, 0)


def wait_all(ref, sem):
    pltpu.make_async_copy(ref, ref, sem).wait()


def whole(
    slots_in, lower_in, weights_in, inverse_in, cot_in, state_in,
    tangent_out, adjoint_out,
    slots, lower, weights, inverse, cot, state, tangent, adjoint,
    to_slot, from_slot, to_row, from_row,
    wx, wz, wo, bx, bk, fx, fz, fo, ax, ab, ao, mx, mo,
    w_sem, b_send, b_recv, fz_send, fz_recv, fx_send, fx_recv,
    az_send, az_recv, ax_send, ax_recv, m_send, m_recv,
    in_sem, out_sem, last_recv,
):
    g, s = lax.axis_index("lat"), lax.axis_index("slab")
    fields, n_lat, n_slab, cap = fx.shape[:4]
    here, per = bk.shape[1], bk.shape[3]
    levels = n_slab * here
    blocks = n_slab * per
    slot_total = n_lat * n_slab * cap
    rows = here * blocks
    low_rows = rows - blocks

    def slab_sends(source, target, send, recv):
        pltpu.make_async_copy(source(s), target(s), recv).start()

        def one(k, carry):
            peer = slab_peer(s, k)
            pltpu.make_async_remote_copy(
                source(peer), target(s), send, recv, device_id=(g, peer), device_id_type=MESH
            ).start()
            return carry

        lax.fori_loop(0, n_slab - 1, one, 0)

    def lat_sends(source, target, send, recv):
        pltpu.make_async_copy(source(g), target(g), recv).start()
        for k in (4, 1, 7, 2, 6, 3, 5):
            peer = (g + k) % n_lat
            pltpu.make_async_remote_copy(
                source(peer), target(g), send, recv, device_id=(peer, s), device_id_type=MESH
            ).start()

    def slot_rows(ref):
        return ref.reshape(fields * slot_total, 128)

    def local_rows(ref):
        return ref.reshape(fields * rows, 128)

    def at_field(f, count):
        return pl.ds(f * count, count)

    inputs = [
        pltpu.make_async_copy(a, b, in_sem.at[i])
        for i, (a, b) in enumerate(
            [
                (weights_in, weights), (inverse_in, inverse), (cot_in, cot), (state_in, state),
                (slots_in, slots), (lower_in, lower),
            ]
        )
    ]
    inputs[4].start()
    inputs[0].start()
    signal_peers(g, s, n_lat, n_slab)
    for i in (1, 2, 5, 3):
        inputs[i].start()
    each = n_slab * cap
    inputs[4].wait()
    inputs[0].wait()
    weight_parts = jnp.concatenate(split(weights[...]), axis=1)
    for k in (4, 1, 7, 2, 6, 3, 5, 0):
        p = (g + k) % n_lat
        here_rows = pl.ds(pl.multiple_of(p * each, each), each)
        table = (iota((each, rows), 0) + p * each == slots[...]).astype(F32).astype(BF16)
        to_slot[here_rows, :] = table
        out = jnp.dot(table, weight_parts, preferred_element_type=F32)
        wx.reshape(slot_total, 128)[here_rows, :] = out[:, :128] + out[:, 128:]
        if k == 4:
            pl.semaphore_wait(pltpu.get_barrier_semaphore(), n_lat + n_slab - 2)
        if k == 0:
            pltpu.make_async_copy(wx.at[p], wz.at[p], w_sem.at[1]).start()
        else:
            pltpu.make_async_remote_copy(
                wx.at[p], wz.at[g], w_sem.at[0], w_sem.at[1], device_id=(p, s), device_id_type=MESH
            ).start()

    def backward(f):
        out = lax.dot_general(
            inverse[f],
            side_by_side(cot, f * per, fields * per, per, levels),
            (((0,), (0,)), ((), ())),
            precision=lax.Precision.HIGHEST,
            preferred_element_type=F32,
        )
        lay_down(local_rows(bx), f * rows, per, per, levels, out)

    def backward_slab(f):
        slab_sends(lambda p: bx.at[f, p], lambda p: bk.at[f, :, p], b_send.at[f], b_recv.at[f])

    def spread(f):
        wait_all(bk.at[f], b_recv.at[f])
        slot_rows(ax)[at_field(f, slot_total), :] = pick(
            to_slot[...], local_rows(bk)[at_field(f, rows), :]
        )

    def gather(f):
        both = jnp.concatenate(
            [
                state[0 : here - 1, f].reshape(low_rows, 128),
                state[1:here, f].reshape(low_rows, 128),
            ],
            axis=1,
        )
        picked = pick(from_row[...], both)
        part = wo.reshape(slot_total, 128)[...]
        slot_rows(fx)[at_field(f, slot_total), :] = (1.0 - part) * picked[:, :128] + part * picked[:, 128:]
        lat_sends(lambda p: fx.at[f, p], lambda p: fz.at[f, p], fz_send.at[f], fz_recv.at[f])

    def pass_on(f):
        wait_all(fz.at[f], fz_recv.at[f])
        slab_sends(lambda p: fz.at[f, :, p], lambda p: fo.at[f, :, p], fx_send.at[f], fx_recv.at[f])

    def arrive(f):
        wait_all(fo.at[f], fx_recv.at[f])
        local_rows(mx)[at_field(f, rows), :] = pick(
            from_slot[...], slot_rows(fo)[at_field(f, slot_total), :]
        )
        slab_sends(lambda p: mx.at[f, :, p], lambda p: mo.at[f, p], m_send.at[f], m_recv.at[f])

    def finish(f):
        wait_all(mo.at[f], m_recv.at[f])
        out = jnp.dot(
            inverse[f],
            side_by_side(local_rows(mo), f * rows, per, per, levels),
            precision=lax.Precision.HIGHEST,
            preferred_element_type=F32,
        )
        lay_down(tangent, f * per, fields * per, per, levels, out)

    def adjoint_slab(f):
        slab_sends(lambda p: ax.at[f, :, p], lambda p: ab.at[f, :, p], ax_send.at[f], ax_recv.at[f])

    def adjoint_lat(f):
        wait_all(ab.at[f], ax_recv.at[f])
        recv = last_recv.at[g] if f == fields - 1 else az_recv.at[f]
        lat_sends(lambda p: ab.at[f, p], lambda p: ao.at[f, p], az_send.at[f], recv)

    def contributions(table, row, part):
        return pick(table, jnp.concatenate([(1.0 - part) * row, part * row], axis=1))

    def scatter(f, sem):
        wait_all(ao.at[f], sem)
        row = slot_rows(ao)[at_field(f, slot_total), :]
        put(f, contributions(to_row[...], row, wo.reshape(slot_total, 128)[...]))

    def scatter_last(f):
        both = jnp.zeros((low_rows, 256), F32)
        for k in (0, 1, 7, 2, 6, 3, 5, 4):
            p = (g + k) % n_lat
            wait_all(ao.at[f, p], last_recv.at[p])
            first = pl.multiple_of(p * each, each)
            both += contributions(
                to_row[:, pl.ds(first, each)],
                slot_rows(ao)[pl.ds(f * slot_total + first, each), :],
                wo.reshape(slot_total, 128)[pl.ds(first, each), :],
            )
        put(f, both)

    def put(f, both):
        low = both[:, :128].reshape(here - 1, blocks, 128)
        high = both[:, 128:].reshape(here - 1, blocks, 128)
        adjoint[0, f] = low[0]
        for l in range(1, here - 1):
            adjoint[l, f] = low[l] + high[l - 1]
        adjoint[here - 1, f] = high[here - 2]
        pltpu.make_async_copy(adjoint.at[:, f], adjoint_out.at[:, f], out_sem.at[f]).start()

    def row_table(p):
        widen = (iota((each, n_slab), 0) // cap == iota((each, n_slab), 1)).astype(F32)
        by_slot = lax.dot_general(
            widen,
            lower[p].astype(F32),
            (((1,), (1,)), ((), ())),
            precision=lax.Precision.HIGHEST,
            preferred_element_type=F32,
        )
        here_only = iota((each, cap), 0) % cap == iota((each, cap), 1)
        ids = jnp.sum(jnp.where(here_only, by_slot, 0.0), axis=1, keepdims=True).astype(jnp.int32)
        return (iota((each, low_rows), 1) == ids).astype(F32)

    early = 2

    def early_lat(f):
        lat_sends(lambda p: ax.at[f, p], lambda p: ab.at[f, p], az_send.at[f], az_recv.at[f])

    def early_slab(f):
        wait_all(ab.at[f], az_recv.at[f])
        slab_sends(lambda p: ab.at[f, :, p], lambda p: ao.at[f, :, p], ax_send.at[f], ax_recv.at[f])

    inputs[1].wait()
    inputs[2].wait()
    inputs[5].wait()
    for f in range(early):
        backward(f)
        backward_slab(f)
    for p in range(n_lat):
        from_row[p * each : (p + 1) * each, :] = row_table(p).astype(BF16)
    spread(0)
    early_lat(0)
    for f in range(1, early):
        spread(f)
    for f in range(early, fields):
        backward(f)
    inputs[3].wait()
    wait_all(wz, w_sem.at[1])
    slab_sends(lambda p: wz.at[:, p], lambda p: wo.at[:, p], w_sem.at[2], w_sem.at[3])
    for f in range(1, early):
        early_lat(f)
    for f in range(early, fields):
        backward_slab(f)
    wait_all(wo, w_sem.at[3])
    for f in range(fields):
        gather(f)
    early_slab(0)
    for f in range(early, fields):
        spread(f)
        adjoint_slab(f)
    for f in range(1, early):
        early_slab(f)
    for p in range(n_lat):
        ids = iota((each, rows), 0) + p * each
        from_slot[:, p * each : (p + 1) * each] = (ids == slots[...]).astype(F32).T.astype(BF16)
        to_row[:, p * each : (p + 1) * each] = row_table(p).T.astype(BF16)
    for f in range(fields):
        pass_on(f)
        if f < fields - early:
            adjoint_lat(early + f)
        if f >= 1:
            arrive(f - 1)
        if f >= 2:
            finish(f - 2)
        if f >= fields - early:
            scatter(f - fields + early, ax_recv.at[f - fields + early])
    arrive(fields - 1)
    finish(fields - 2)
    finish(fields - 1)
    tangent_copy = pltpu.make_async_copy(tangent, tangent_out, out_sem.at[fields])
    tangent_copy.start()
    for f in range(early, fields - 1):
        scatter(f, az_recv.at[f])
    scatter_last(fields - 1)

    wait_all(wz.at[: n_lat - 1], w_sem.at[0])
    wait_all(wo.at[:, : n_slab - 1], w_sem.at[2])
    for f in range(fields):
        wait_all(bx.at[f, : n_slab - 1], b_send.at[f])
        wait_all(fz.at[f, : n_lat - 1], fz_send.at[f])
        wait_all(fo.at[f, :, : n_slab - 1], fx_send.at[f])
        wait_all(mo.at[f, : n_slab - 1], m_send.at[f])
        wait_all(ao.at[f, : n_lat - 1], az_send.at[f])
        wait_all(ab.at[f, :, : n_slab - 1], ax_send.at[f])
    tangent_copy.wait()
    for f in range(fields):
        pltpu.make_async_copy(adjoint.at[:, f], adjoint_out.at[:, f], out_sem.at[f]).wait()


def body(field_state, cotangent, vertical_weight, diffusion_inverse, source_row, dest_slot):
    _, here, blocks, fields, width = field_state.shape
    levels, per = cotangent.shape[1], cotangent.shape[2]
    n_lat, n_slab, cap = source_row.shape[2:]
    rows = here * blocks
    slot_total = n_lat * n_slab * cap
    low_rows = rows - blocks
    dma = pltpu.SemaphoreType.DMA

    state = field_state.transpose(0, 1, 3, 2, 4).reshape(here, fields, blocks, width)
    cot = cotangent.transpose(0, 1, 3, 2, 4).reshape(levels * fields * per, width)
    lower = source_row.reshape(n_lat, n_slab, cap).transpose(0, 2, 1)
    anywhere = pl.BlockSpec(memory_space=pl.ANY)
    slot_array = pltpu.VMEM((fields, n_lat, n_slab, cap, width), F32)
    weight_array = pltpu.VMEM((n_lat, n_slab, cap, width), F32)
    by_level = pltpu.VMEM((fields, here, n_slab, per, width), F32)
    by_block = pltpu.VMEM((fields, n_slab, here, per, width), F32)

    shapes = (
        jax.ShapeDtypeStruct((levels * fields * per, width), F32),
        jax.ShapeDtypeStruct((here, fields, blocks, width), F32),
    )
    results = pl.pallas_call(
        whole,
        out_shape=shapes,
        in_specs=[anywhere] * 6,
        out_specs=(anywhere, anywhere),
        scratch_shapes=[
            pltpu.VMEM((1, rows), jnp.int32),
            pltpu.VMEM((n_lat, cap, n_slab), jnp.int32),
            pltpu.VMEM((rows, width), F32),
            pltpu.VMEM((fields, levels, levels), F32),
            pltpu.VMEM((levels * fields * per, width), F32),
            pltpu.VMEM((here, fields, blocks, width), F32),
            pltpu.VMEM((levels * fields * per, width), F32),
            pltpu.VMEM((here, fields, blocks, width), F32),
            pltpu.VMEM((slot_total, rows), BF16),
            pltpu.VMEM((rows, slot_total), BF16),
            pltpu.VMEM((low_rows, slot_total), BF16),
            pltpu.VMEM((slot_total, low_rows), BF16),
            weight_array, weight_array, weight_array,
            by_block, by_level,
            slot_array, slot_array, slot_array,
            slot_array, slot_array, slot_array,
            by_level, by_block,
            dma((4,)),
        ] + [dma((fields,))] * 12 + [dma((6,)), dma((fields + 1,)), dma((n_lat,))],
        compiler_params=pltpu.CompilerParams(
            vmem_limit_bytes=VMEM_LIMIT, collective_id=0, has_side_effects=True
        ),
    )(
        *(
            pltpu.with_memory_space_constraint(part, pltpu.HBM)
            for part in (
                dest_slot.reshape(1, rows), lower,
                vertical_weight.reshape(rows, width), diffusion_inverse[0], cot, state,
            )
        )
    )
    tangent, adjoint = results
    tangent = tangent.reshape(1, levels, fields, per, width).transpose(0, 1, 3, 2, 4)
    adjoint = adjoint.reshape(1, here, fields, blocks, width).transpose(0, 1, 3, 2, 4)
    return tangent, adjoint


def solution(mesh):
    placed = (
        P("lat", "slab", None, None, None),
        P("lat", None, "slab", None, None),
        P("lat", "slab", None, None),
        P("lat", None, None, None),
        P("lat", "slab", None, None, None),
        P("lat", "slab", None),
    )
    return jax.shard_map(
        body,
        mesh=mesh,
        in_specs=placed,
        out_specs=(P("lat", None, "slab", None, None), P("lat", "slab", None, None, None)),
        check_vma=False,
    )
```

```python
import functools

import jax
import jax.numpy as jnp
from jax import lax
from jax.experimental import pallas as pl
from jax.experimental.pallas import tpu as pltpu
from jax.sharding import PartitionSpec as P

MESH = pl.DeviceIdType.MESH
VMEM_LIMIT = 40 << 20
F32 = jnp.float32
BF16 = jnp.bfloat16


def split(values):
    high = values.astype(BF16)
    return high, (values - high.astype(F32)).astype(BF16)


def pick(table, values):
    width = values.shape[1]
    out = jnp.dot(table, jnp.concatenate(split(values), axis=1), preferred_element_type=F32)
    return out[:, :width] + out[:, width:]


def iota(shape, axis):
    return lax.broadcasted_iota(jnp.int32, shape, axis)


def slab_peer(s, t):
    i = t + (t + 29) // 32
    q, j = i % 4, (i // 4) % 4
    dx = (q // 2) * (6 - 2 * q) + (1 - q // 2) * (1 + 2 * q)
    dy = dx + j + (j // 2) * (1 - 2 * (j % 2))
    x, y, core = s // 8, (s // 2) % 4, s % 2
    return ((x + dx) % 4) * 8 + ((y + dy) % 4) * 2 + (core + i // 16) % 2


def side_by_side(view, first, stride, per, levels):
    parts = [view[pl.ds(first + b, levels, stride=stride), :] for b in range(per)]
    return jnp.concatenate(parts, axis=1)


def lay_down(view, first, stride, per, levels, values):
    for b in range(per):
        view[pl.ds(first + b, levels, stride=stride), :] = values[:, b * 128 : (b + 1) * 128]


def signal_peers(g, s, n_lat, n_slab):
    bar = pltpu.get_barrier_semaphore()
    for k in range(1, n_lat):
        pl.semaphore_signal(bar, inc=1, device_id=((g + k) % n_lat, s), device_id_type=MESH)

    def one(k, carry):
        pl.semaphore_signal(bar, inc=1, device_id=(g, slab_peer(s, k)), device_id_type=MESH)
        return carry

    lax.fori_loop(0, n_slab - 1, one, 0)


def wait_all(ref, sem):
    pltpu.make_async_copy(ref, ref, sem).wait()


def whole(
    slots_in, lower_in, weights_in, inverse_in, cot_in, state_in,
    tangent_out, adjoint_out,
    slots, lower, weights, inverse, cot, state, tangent, adjoint,
    to_slot, from_slot, to_row, from_row,
    wx, wz, wo, bx, bk, fx, fz, fo, ax, ab, ao, mx, mo,
    w_sem, b_send, b_recv, fz_send, fz_recv, fx_send, fx_recv,
    az_send, az_recv, ax_send, ax_recv, m_send, m_recv,
    in_sem, out_sem, last_recv,
):
    g, s = lax.axis_index("lat"), lax.axis_index("slab")
    fields, n_lat, n_slab, cap = fx.shape[:4]
    here, per = bk.shape[1], bk.shape[3]
    levels = n_slab * here
    blocks = n_slab * per
    slot_total = n_lat * n_slab * cap
    rows = here * blocks
    low_rows = rows - blocks

    def slab_sends(source, target, send, recv):
        pltpu.make_async_copy(source(s), target(s), recv).start()

        def one(k, carry):
            peer = slab_peer(s, k)
            pltpu.make_async_remote_copy(
                source(peer), target(s), send, recv, device_id=(g, peer), device_id_type=MESH
            ).start()
            return carry

        lax.fori_loop(0, n_slab - 1, one, 0)

    def lat_sends(source, target, send, recv):
        pltpu.make_async_copy(source(g), target(g), recv).start()
        for k in (4, 1, 7, 2, 6, 3, 5):
            peer = (g + k) % n_lat
            pltpu.make_async_remote_copy(
                source(peer), target(g), send, recv, device_id=(peer, s), device_id_type=MESH
            ).start()

    def slot_rows(ref):
        return ref.reshape(fields * slot_total, 128)

    def local_rows(ref):
        return ref.reshape(fields * rows, 128)

    def at_field(f, count):
        return pl.ds(f * count, count)

    inputs = [
        pltpu.make_async_copy(a, b, in_sem.at[i])
        for i, (a, b) in enumerate(
            [
                (weights_in, weights), (inverse_in, inverse), (cot_in, cot), (state_in, state),
                (slots_in, slots), (lower_in, lower),
            ]
        )
    ]
    inputs[4].start()
    inputs[0].start()
    signal_peers(g, s, n_lat, n_slab)
    for i in (1, 2, 5, 3):
        inputs[i].start()
    each = n_slab * cap
    inputs[4].wait()
    inputs[0].wait()
    weight_parts = jnp.concatenate(split(weights[...]), axis=1)
    for k in (4, 1, 7, 2, 6, 3, 5, 0):
        p = (g + k) % n_lat
        here_rows = pl.ds(pl.multiple_of(p * each, each), each)
        table = (iota((each, rows), 0) + p * each == slots[...]).astype(F32).astype(BF16)
        to_slot[here_rows, :] = table
        out = jnp.dot(table, weight_parts, preferred_element_type=F32)
        wx.reshape(slot_total, 128)[here_rows, :] = out[:, :128] + out[:, 128:]
        if k == 4:
            pl.semaphore_wait(pltpu.get_barrier_semaphore(), n_lat + n_slab - 2)
        if k == 0:
            pltpu.make_async_copy(wx.at[p], wz.at[p], w_sem.at[1]).start()
        else:
            pltpu.make_async_remote_copy(
                wx.at[p], wz.at[g], w_sem.at[0], w_sem.at[1], device_id=(p, s), device_id_type=MESH
            ).start()

    def backward(f):
        out = lax.dot_general(
            inverse[f],
            side_by_side(cot, f * per, fields * per, per, levels),
            (((0,), (0,)), ((), ())),
            precision=lax.Precision.HIGHEST,
            preferred_element_type=F32,
        )
        lay_down(local_rows(bx), f * rows, per, per, levels, out)

    def backward_slab(f):
        slab_sends(lambda p: bx.at[f, p], lambda p: bk.at[f, :, p], b_send.at[f], b_recv.at[f])

    def spread(f):
        wait_all(bk.at[f], b_recv.at[f])
        slot_rows(ax)[at_field(f, slot_total), :] = pick(
            to_slot[...], local_rows(bk)[at_field(f, rows), :]
        )

    def gather(f):
        both = jnp.concatenate(
            [
                state[0 : here - 1, f].reshape(low_rows, 128),
                state[1:here, f].reshape(low_rows, 128),
            ],
            axis=1,
        )
        picked = pick(from_row[...], both)
        part = wo.reshape(slot_total, 128)[...]
        slot_rows(fx)[at_field(f, slot_total), :] = (1.0 - part) * picked[:, :128] + part * picked[:, 128:]
        lat_sends(lambda p: fx.at[f, p], lambda p: fz.at[f, p], fz_send.at[f], fz_recv.at[f])

    def pass_on(f):
        wait_all(fz.at[f], fz_recv.at[f])
        slab_sends(lambda p: fz.at[f, :, p], lambda p: fo.at[f, :, p], fx_send.at[f], fx_recv.at[f])

    def arrive(f):
        wait_all(fo.at[f], fx_recv.at[f])
        local_rows(mx)[at_field(f, rows), :] = pick(
            from_slot[...], slot_rows(fo)[at_field(f, slot_total), :]
        )
        slab_sends(lambda p: mx.at[f, :, p], lambda p: mo.at[f, p], m_send.at[f], m_recv.at[f])

    def finish(f):
        wait_all(mo.at[f], m_recv.at[f])
        out = jnp.dot(
            inverse[f],
            side_by_side(local_rows(mo), f * rows, per, per, levels),
            precision=lax.Precision.HIGHEST,
            preferred_element_type=F32,
        )
        lay_down(tangent, f * per, fields * per, per, levels, out)

    def adjoint_slab(f):
        slab_sends(lambda p: ax.at[f, :, p], lambda p: ab.at[f, :, p], ax_send.at[f], ax_recv.at[f])

    def adjoint_lat(f):
        wait_all(ab.at[f], ax_recv.at[f])
        recv = last_recv.at[g] if f == fields - 1 else az_recv.at[f]
        lat_sends(lambda p: ab.at[f, p], lambda p: ao.at[f, p], az_send.at[f], recv)

    def contributions(table, row, part):
        return pick(table, jnp.concatenate([(1.0 - part) * row, part * row], axis=1))

    def scatter(f, sem):
        wait_all(ao.at[f], sem)
        row = slot_rows(ao)[at_field(f, slot_total), :]
        put(f, contributions(to_row[...], row, wo.reshape(slot_total, 128)[...]))

    def scatter_last(f):
        both = jnp.zeros((low_rows, 256), F32)
        for k in (0, 1, 7, 2, 6, 3, 5, 4):
            p = (g + k) % n_lat
            wait_all(ao.at[f, p], last_recv.at[p])
            first = pl.multiple_of(p * each, each)
            both += contributions(
                to_row[:, pl.ds(first, each)],
                slot_rows(ao)[pl.ds(f * slot_total + first, each), :],
                wo.reshape(slot_total, 128)[pl.ds(first, each), :],
            )
        put(f, both)

    def put(f, both):
        low = both[:, :128].reshape(here - 1, blocks, 128)
        high = both[:, 128:].reshape(here - 1, blocks, 128)
        adjoint[0, f] = low[0]
        for l in range(1, here - 1):
            adjoint[l, f] = low[l] + high[l - 1]
        adjoint[here - 1, f] = high[here - 2]
        pltpu.make_async_copy(adjoint.at[:, f], adjoint_out.at[:, f], out_sem.at[f]).start()

    def row_table(p):
        widen = (iota((each, n_slab), 0) // cap == iota((each, n_slab), 1)).astype(F32)
        by_slot = lax.dot_general(
            widen,
            lower[p].astype(F32),
            (((1,), (1,)), ((), ())),
            precision=lax.Precision.HIGHEST,
            preferred_element_type=F32,
        )
        here_only = iota((each, cap), 0) % cap == iota((each, cap), 1)
        ids = jnp.sum(jnp.where(here_only, by_slot, 0.0), axis=1, keepdims=True).astype(jnp.int32)
        return (iota((each, low_rows), 1) == ids).astype(F32)

    early = 2

    def early_lat(f):
        lat_sends(lambda p: ax.at[f, p], lambda p: ab.at[f, p], az_send.at[f], az_recv.at[f])

    def early_slab(f):
        wait_all(ab.at[f], az_recv.at[f])
        slab_sends(lambda p: ab.at[f, :, p], lambda p: ao.at[f, :, p], ax_send.at[f], ax_recv.at[f])

    inputs[1].wait()
    inputs[2].wait()
    inputs[5].wait()
    for f in range(early):
        backward(f)
        backward_slab(f)
    for p in range(n_lat):
        from_row[p * each : (p + 1) * each, :] = row_table(p).astype(BF16)
    spread(0)
    early_lat(0)
    for f in range(1, early):
        spread(f)
    for f in range(early, fields):
        backward(f)
    inputs[3].wait()
    wait_all(wz, w_sem.at[1])
    slab_sends(lambda p: wz.at[:, p], lambda p: wo.at[:, p], w_sem.at[2], w_sem.at[3])
    for f in range(1, early):
        early_lat(f)
    for f in range(early, fields):
        backward_slab(f)
    wait_all(wo, w_sem.at[3])
    for f in range(fields):
        gather(f)
    early_slab(0)
    for f in range(early, fields):
        spread(f)
        adjoint_slab(f)
    for f in range(1, early):
        early_slab(f)
    for p in range(n_lat):
        ids = iota((each, rows), 0) + p * each
        from_slot[:, p * each : (p + 1) * each] = (ids == slots[...]).astype(F32).T.astype(BF16)
        to_row[:, p * each : (p + 1) * each] = row_table(p).T.astype(BF16)
    for f in range(fields):
        pass_on(f)
        if f < fields - early:
            adjoint_lat(early + f)
        if f >= 1:
            arrive(f - 1)
        if f >= 2:
            finish(f - 2)
        if f >= fields - early:
            scatter(f - fields + early, ax_recv.at[f - fields + early])
    arrive(fields - 1)
    finish(fields - 2)
    finish(fields - 1)
    tangent_copy = pltpu.make_async_copy(tangent, tangent_out, out_sem.at[fields])
    tangent_copy.start()
    for f in range(early, fields - 1):
        scatter(f, az_recv.at[f])
    wait_all(wz.at[: n_lat - 1], w_sem.at[0])
    wait_all(wo.at[:, : n_slab - 1], w_sem.at[2])
    for f in range(fields):
        wait_all(bx.at[f, : n_slab - 1], b_send.at[f])
        wait_all(fz.at[f, : n_lat - 1], fz_send.at[f])
        wait_all(fo.at[f, :, : n_slab - 1], fx_send.at[f])
        wait_all(mo.at[f, : n_slab - 1], m_send.at[f])
        if f < fields - 1:
            wait_all(ao.at[f, : n_lat - 1], az_send.at[f])
        wait_all(ab.at[f, :, : n_slab - 1], ax_send.at[f])
    tangent_copy.wait()
    scatter_last(fields - 1)
    wait_all(ao.at[fields - 1, : n_lat - 1], az_send.at[fields - 1])
    for f in range(fields):
        pltpu.make_async_copy(adjoint.at[:, f], adjoint_out.at[:, f], out_sem.at[f]).wait()


def body(field_state, cotangent, vertical_weight, diffusion_inverse, source_row, dest_slot):
    _, here, blocks, fields, width = field_state.shape
    levels, per = cotangent.shape[1], cotangent.shape[2]
    n_lat, n_slab, cap = source_row.shape[2:]
    rows = here * blocks
    slot_total = n_lat * n_slab * cap
    low_rows = rows - blocks
    dma = pltpu.SemaphoreType.DMA

    state = field_state.transpose(0, 1, 3, 2, 4).reshape(here, fields, blocks, width)
    cot = cotangent.transpose(0, 1, 3, 2, 4).reshape(levels * fields * per, width)
    lower = source_row.reshape(n_lat, n_slab, cap).transpose(0, 2, 1)
    anywhere = pl.BlockSpec(memory_space=pl.ANY)
    slot_array = pltpu.VMEM((fields, n_lat, n_slab, cap, width), F32)
    weight_array = pltpu.VMEM((n_lat, n_slab, cap, width), F32)
    by_level = pltpu.VMEM((fields, here, n_slab, per, width), F32)
    by_block = pltpu.VMEM((fields, n_slab, here, per, width), F32)

    shapes = (
        jax.ShapeDtypeStruct((levels * fields * per, width), F32),
        jax.ShapeDtypeStruct((here, fields, blocks, width), F32),
    )
    results = pl.pallas_call(
        whole,
        out_shape=shapes,
        in_specs=[anywhere] * 6,
        out_specs=(anywhere, anywhere),
        scratch_shapes=[
            pltpu.VMEM((1, rows), jnp.int32),
            pltpu.VMEM((n_lat, cap, n_slab), jnp.int32),
            pltpu.VMEM((rows, width), F32),
            pltpu.VMEM((fields, levels, levels), F32),
            pltpu.VMEM((levels * fields * per, width), F32),
            pltpu.VMEM((here, fields, blocks, width), F32),
            pltpu.VMEM((levels * fields * per, width), F32),
            pltpu.VMEM((here, fields, blocks, width), F32),
            pltpu.VMEM((slot_total, rows), BF16),
            pltpu.VMEM((rows, slot_total), BF16),
            pltpu.VMEM((low_rows, slot_total), BF16),
            pltpu.VMEM((slot_total, low_rows), BF16),
            weight_array, weight_array, weight_array,
            by_block, by_level,
            slot_array, slot_array, slot_array,
            slot_array, slot_array, slot_array,
            by_level, by_block,
            dma((4,)),
        ] + [dma((fields,))] * 12 + [dma((6,)), dma((fields + 1,)), dma((n_lat,))],
        compiler_params=pltpu.CompilerParams(
            vmem_limit_bytes=VMEM_LIMIT, collective_id=0, has_side_effects=True
        ),
    )(
        *(
            pltpu.with_memory_space_constraint(part, pltpu.HBM)
            for part in (
                dest_slot.reshape(1, rows), lower,
                vertical_weight.reshape(rows, width), diffusion_inverse[0], cot, state,
            )
        )
    )
    tangent, adjoint = results
    tangent = tangent.reshape(1, levels, fields, per, width).transpose(0, 1, 3, 2, 4)
    adjoint = adjoint.reshape(1, here, fields, blocks, width).transpose(0, 1, 3, 2, 4)
    return tangent, adjoint


def solution(mesh):
    placed = (
        P("lat", "slab", None, None, None),
        P("lat", None, "slab", None, None),
        P("lat", "slab", None, None),
        P("lat", None, None, None),
        P("lat", "slab", None, None, None),
        P("lat", "slab", None),
    )
    return jax.shard_map(
        body,
        mesh=mesh,
        in_specs=placed,
        out_specs=(P("lat", None, "slab", None, None), P("lat", "slab", None, None, None)),
        check_vma=False,
    )
```
